32 devices in a mesh: expert: 4 (over y, core), row: 8 (over z, x).
Axes of the slice: x: 2, y: 2, z: 4, core: 2. Of those that a mesh axis runs over, the one named last changes fastest.
Arguments:
- sampled: int32 [4, 32], P('expert'), may hold values from 0 to 31, each once within a row
- refresh: int32 [64], P('expert'), may hold values 0 or 1
- momentum_bank: bfloat16 [128, 2048, 512], P('expert', 'row'), may hold values from -6 to 6
- weights: bfloat16 [64, 2048, 512], P('expert', 'row'), may hold values from -6 to 6
- grads: bfloat16 [64, 2048, 512], P('expert', 'row'), may hold values from -6 to 6
- basis: float32 [64, 2048, 64], P('expert', 'row'), may hold values from -0.125 to 0.125
Outputs:
- new_bank: bfloat16 [128, 2048, 512], P('expert', 'row')
- new_weights: bfloat16 [64, 2048, 512], P('expert', 'row')
The draws below stay inside these ranges and needn't reach their ends.
Inputs may be any that keep to these rules, and one draw needn't show every extreme that they name: Each row of sampled names every number of 0 to 31 once.
All inputs are finite; a program needn't handle non-finite values. No bound on the sum of `refresh` on one device may be relied on, other than what follows from the above.
Results may differ from the reference program's by a relative error of at most 0.0045.
Values may be sent and summed in bfloat16 or wider, within the bound.
A program may use at most 128 MiB of HBM per device.

```python
import math
import jax
import jax.numpy as jnp
from jax import lax

D = 2048
FF = 512
RANK = 64
E_LOC = 32
ITERS = 3
S_LOC = 16
GROUPS = 4
EXPERTS = 128
SAMPLED = 64


def touch_ends(entries, rng, smallest, largest):
    place = [jax.random.randint(jax.random.fold_in(rng, axis), (), 0, length) for axis, length in enumerate(entries.shape)]
    main_axis = entries.shape.index(max(entries.shape))
    beside = place[:main_axis] + [(place[main_axis] + 1) % entries.shape[main_axis]] + place[main_axis + 1:]
    return entries.at[tuple(place)].set(smallest).at[tuple(beside)].set(largest)


def levels(rng, dims, split, low, top_value):
    factor_of, own = 1.0, jax.random.fold_in(rng, 6)
    for position, blocks in split:
        heights = jnp.exp(jax.random.uniform(jax.random.fold_in(own, position), (blocks,), jnp.float32, low / len(split), top_value / len(split)))
        factor_of = factor_of * jnp.repeat(heights, dims[position] // blocks).reshape([-1 if axis == position else 1 for axis in range(len(dims))])
    return factor_of


def normal_values(stream_key, dims, width, reach, split=(), held_as=jnp.bfloat16):
    values = jax.random.normal(stream_key, dims, jnp.float32) * width
    if len(split) > 0:
        values = levels(stream_key, dims, split, -0.22, 0.18) * values
    return jnp.clip(values, min=-reach, max=reach).astype(held_as)


def setup_inputs(seed: int = 0) -> dict:
    seeds = jax.random.split(jax.random.key(seed), 7)
    sampled = jax.vmap(lambda own: jax.random.permutation(own, E_LOC))(jax.random.split(seeds[0], GROUPS)).reshape((GROUPS, E_LOC)).astype(jnp.int32)
    refresh = touch_ends((jax.random.randint(seeds[1], (SAMPLED,), 0, 3) < 1).astype(jnp.int32), jax.random.fold_in(seeds[1], 1), 0, 1)
    momentum_bank = normal_values(seeds[2], (EXPERTS, D, FF), 1.0, 6.0, ((0, 4), (1, 8)))
    weights = normal_values(seeds[3], (SAMPLED, D, FF), 1.0, 6.0, ((0, 4), (1, 8)))
    grads = normal_values(seeds[4], (SAMPLED, D, FF), 1.0, 6.0, ((0, 4), (1, 8)))
    basis = normal_values(seeds[5], (SAMPLED, D, RANK), D ** -0.5, 0.125, ((0, 4), (1, 8)), jnp.float32)
    return {"sampled": sampled, "refresh": refresh, "momentum_bank": momentum_bank, "weights": weights, "grads": grads, "basis": basis}


momentum_decay = 0.9
residual_weight = 2.0
step_rate = 0.5
decay_rate = 0.1
coef_first = 3.4445
coef_second = -4.775
coef_third = 2.0315
epsilon = 1e-07

def newton(matrix):
    values = matrix.astype(jnp.float32)
    total_norm = jnp.sqrt(jnp.sum(values * values)) + epsilon
    iterate = (values / total_norm).astype(jnp.bfloat16)
    for sweep in range(ITERS):
        current = iterate.astype(jnp.float32)
        gram = jnp.dot(current.T, current, precision=lax.Precision.HIGHEST).astype(jnp.bfloat16)
        gram_full = lax.optimization_barrier(gram).astype(jnp.float32)
        square = jnp.dot(gram_full, gram_full, precision=lax.Precision.HIGHEST)
        poly = (coef_second * gram_full + coef_third * square).astype(jnp.bfloat16)
        poly_full = lax.optimization_barrier(poly).astype(jnp.float32)
        iterate = (coef_first * current + jnp.dot(current, poly_full, precision=lax.Precision.HIGHEST)).astype(jnp.bfloat16)
    return iterate

def reference(sampled, refresh, momentum_bank, weights, grads, basis):
    groups = sampled.shape[0]
    offsets = (jnp.arange(groups, dtype=jnp.int32) * E_LOC)[:, None]
    experts_hit = (sampled[:, :S_LOC].astype(jnp.int32) + offsets).reshape(-1).astype(jnp.int32)
    scale_step = step_rate * 0.2 * math.sqrt(max(D, FF))

    def single(items):
        index, weight_flag, weight_now, gradient, projector = items
        old = momentum_bank[index].astype(jnp.float32)
        grad_full = gradient.astype(jnp.float32)
        proj = jnp.dot(projector.T, grad_full, precision=lax.Precision.HIGHEST)
        low = jnp.dot(projector, proj, precision=lax.Precision.HIGHEST)
        mom = (momentum_decay * old + low + residual_weight * weight_flag * (grad_full - low)).astype(jnp.bfloat16)
        ortho = newton(mom)
        updated = weight_now.astype(jnp.float32) * (1.0 - step_rate * decay_rate) - scale_step * ortho.astype(jnp.float32)
        return (mom, updated.astype(jnp.bfloat16))
    moms, new_weights = lax.map(single, (experts_hit, refresh.astype(jnp.float32), weights, grads, basis))
    new_bank = momentum_bank.at[experts_hit].set(moms)
    return (new_bank, new_weights)
```

```python
import math

import jax
import jax.numpy as jnp
from jax import lax
from jax.sharding import PartitionSpec as P

D = 2048
FF = 512
ITERS = 3


momentum_decay = 0.9
residual_weight = 2.0
step_rate = 0.5
decay_rate = 0.1
coef_first = 3.4445
coef_second = -4.775
coef_third = 2.0315
epsilon = 1e-07
TILE = 128


def pack_upper(full):
    width = full.shape[-1]
    return jnp.concatenate(
        [full[:, at : at + TILE, at:] for at in range(0, width, TILE)], axis=2
    )


def unpack_upper(packed, width):
    rows = []
    offset = 0
    tiles = {}
    count = width // TILE
    for i in range(count):
        for j in range(i, count):
            tile = packed[:, :, offset : offset + TILE]
            tiles[i, j] = tile
            if j > i:
                tiles[j, i] = jnp.swapaxes(tile, 1, 2)
            offset += TILE
    for i in range(count):
        rows.append(jnp.concatenate([tiles[i, j] for j in range(count)], axis=2))
    return jnp.concatenate(rows, axis=1)


def mm(a, b):
    return jnp.einsum(
        "mij,mjk->mik",
        a.astype(jnp.bfloat16),
        b.astype(jnp.bfloat16),
        preferred_element_type=jnp.float32,
    )


def factors(gram):
    width = gram.shape[-1]
    eye = jnp.eye(width, dtype=jnp.float32)
    total = jnp.sum(gram * eye, axis=(1, 2), keepdims=True)
    inverse = 1.0 / (jnp.sqrt(total) + epsilon)
    a = gram * inverse * inverse
    q = None
    for sweep in range(ITERS):
        poly = coef_second * a + coef_third * mm(a, a)
        q = coef_first * eye + poly if q is None else coef_first * q + mm(q, poly)
        if sweep < ITERS - 1:
            half = coef_first * a + mm(a, poly)
            a = coef_first * half + mm(poly, half)
    return q * inverse


def shards(sampled, refresh, momentum_bank, weights, grads, basis):
    group_count = weights.shape[0]
    width = weights.shape[2]
    chosen = sampled[0, :group_count]
    old = momentum_bank[chosen].astype(jnp.float32)
    basis_high = basis.astype(jnp.bfloat16)
    partial_sum = jnp.einsum("srk,srf->skf", basis_high, grads, preferred_element_type=jnp.float32)
    proj = lax.psum(partial_sum.astype(jnp.bfloat16), "row")
    low = jnp.einsum("srk,skf->srf", basis_high, proj, preferred_element_type=jnp.float32)
    weight_flag = refresh.astype(jnp.float32)[:, None, None]
    grad_full = grads.astype(jnp.float32)
    mom = (momentum_decay * old + low + residual_weight * weight_flag * (grad_full - low)).astype(
        jnp.bfloat16
    )
    new_bank = momentum_bank.at[chosen].set(mom)
    partial_gram = jnp.einsum("srf,srg->sfg", mom, mom, preferred_element_type=jnp.float32)
    packed = pack_upper(partial_gram).astype(jnp.bfloat16)
    summed = lax.psum_scatter(packed, "row", scatter_dimension=0, tiled=True)
    q = factors(unpack_upper(summed.astype(jnp.float32), width))
    sent = pack_upper(q.astype(jnp.bfloat16))
    everyone = lax.all_gather(sent, "row", axis=0, tiled=True)
    q_full = unpack_upper(everyone, width)
    ortho = jnp.einsum("srf,sfg->srg", mom, q_full, preferred_element_type=jnp.float32)
    scale_step = step_rate * 0.2 * math.sqrt(max(D, FF))
    updated = weights.astype(jnp.float32) * (1.0 - step_rate * decay_rate) - scale_step * ortho
    return (new_bank, updated.astype(jnp.bfloat16))


def solution(mesh):
    in_specs = (
        P("expert", None),
        P("expert"),
        P("expert", "row", None),
        P("expert", "row", None),
        P("expert", "row", None),
        P("expert", "row", None),
    )
    out_specs = (P("expert", "row", None), P("expert", "row", None))
    return jax.shard_map(shards, mesh=mesh, in_specs=in_specs, out_specs=out_specs, check_vma=False)
```

```python
import functools
import math

import jax
import jax.numpy as jnp
from jax import lax
from jax.experimental import pallas as pl
from jax.experimental.pallas import tpu as pltpu
from jax.sharding import PartitionSpec as P

D = 2048
FF = 512
ITERS = 3


momentum_decay = 0.9
residual_weight = 2.0
step_rate = 0.5
decay_rate = 0.1
coef_first = 3.4445
coef_second = -4.775
coef_third = 2.0315
epsilon = 1e-07
TILE = 128
MESH = pl.DeviceIdType.MESH
F32 = jnp.float32
BF16 = jnp.bfloat16


def grid_of(owners):
    inner = 2 if owners % 2 == 0 and owners <= 8 else 4
    return owners // inner, inner


class Plan:
    def __init__(self, owners):
        self.outer, self.inner = grid_of(owners)
        me = lax.axis_index("row")
        self.o = me // self.inner
        self.i = lax.rem(me, self.inner)

    def o_at(self, d):
        return lax.rem(self.o + d, self.outer)

    def i_at(self, d):
        return lax.rem(self.i + d, self.inner)

    def row(self, o, i):
        return o * self.inner + i

    def barrier(self):
        sem = pltpu.get_barrier_semaphore()
        for d in range(1, self.inner):
            pl.semaphore_signal(
                sem, inc=1, device_id={"row": self.row(self.o, self.i_at(d))}, device_id_type=MESH
            )
        for d in range(1, self.outer):
            pl.semaphore_signal(
                sem, inc=1, device_id={"row": self.row(self.o_at(d), self.i)}, device_id_type=MESH
            )
        pl.semaphore_wait(sem, self.inner + self.outer - 2)


def remote(src, dst, send, recv, target):
    return pltpu.make_async_remote_copy(
        src_ref=src,
        dst_ref=dst,
        send_sem=send,
        recv_sem=recv,
        device_id={"row": target},
        device_id_type=MESH,
    )


class SumScatter:
    def __init__(self, plan, per, x, near, far, sums, sems):
        self.plan, self.per, self.x, self.near, self.far, self.sums = plan, per, x, near, far, sums
        self.s1, self.r1, self.s2, self.r2 = sems
        self.second = {}

    @staticmethod
    def scratch(owners, per, tile):
        outer, inner = grid_of(owners)
        dma = pltpu.SemaphoreType.DMA
        return [
            pltpu.VMEM((inner - 1, outer, per) + tile, BF16),
            pltpu.VMEM((outer - 1, per) + tile, BF16),
            pltpu.VMEM((outer, per) + tile, BF16),
            dma((inner - 1, outer, per)),
            dma((inner - 1, outer, per)),
            dma((outer - 1, per)),
            dma((outer - 1, per)),
        ]

    def steps(self):
        return [(p, d) for p in range(self.per) for d in list(range(1, self.plan.outer)) + [0]]

    def first_copy(self, p, d, e):
        plan = self.plan
        target = plan.row(plan.o, plan.i_at(e))
        return remote(
            self.x.at[plan.row(plan.o_at(d), plan.i_at(e)) * self.per + p],
            self.near.at[e - 1, d, p],
            self.s1.at[e - 1, d, p],
            self.r1.at[e - 1, d, p],
            target,
        )

    def start(self):
        for p, d in self.steps():
            for e in range(1, self.plan.inner):
                self.first_copy(p, d, e).start()

    def partial(self, p, d):
        plan = self.plan
        total = self.x[plan.row(plan.o_at(d), plan.i) * self.per + p].astype(F32)
        for e in range(1, plan.inner):
            self.first_copy(p, d, e).wait_recv()
            total = total + self.near[e - 1, d, p].astype(F32)
        return total

    def second_copy(self, p, d):
        plan = self.plan
        return remote(
            self.sums.at[d, p],
            self.far.at[d - 1, p],
            self.s2.at[d - 1, p],
            self.r2.at[d - 1, p],
            plan.row(plan.o_at(d), plan.i),
        )

    def forward(self, p):
        for d in range(1, self.plan.outer):
            self.sums[d, p] = self.partial(p, d).astype(BF16)
            self.second_copy(p, d).start()
        self.sums[0, p] = self.partial(p, 0).astype(BF16)

    def total(self, p):
        value = self.sums[0, p].astype(F32)
        for d in range(1, self.plan.outer):
            self.second_copy(p, d).wait_recv()
            value = value + self.far[d - 1, p].astype(F32)
        return value

    def finish(self):
        for p, d in self.steps():
            for e in range(1, self.plan.inner):
                self.first_copy(p, d, e).wait_send()
            if d:
                self.second_copy(p, d).wait_send()


class Gather:
    def __init__(self, plan, per, out, sems):
        self.plan, self.per, self.out = plan, per, out
        self.s1, self.r1, self.s2, self.r2 = sems

    @staticmethod
    def scratch(owners, per):
        outer, inner = grid_of(owners)
        dma = pltpu.SemaphoreType.DMA
        return [
            dma((outer - 1, per)),
            dma((outer - 1, per)),
            dma((inner - 1, outer, per)),
            dma((inner - 1, outer, per)),
        ]

    def place(self, o, p):
        return self.out.at[self.plan.row(o, self.plan.i) * self.per + p]

    def first_copy(self, p, d):
        plan = self.plan
        own = self.place(plan.o, p)
        return remote(own, own, self.s1.at[d - 1, p], self.r1.at[d - 1, p], plan.row(plan.o_at(d), plan.i))

    def second_copy(self, p, d, e):
        plan = self.plan
        own = self.place(plan.o_at(plan.outer - d), p)
        return remote(
            own, own, self.s2.at[e - 1, d, p], self.r2.at[e - 1, d, p], plan.row(plan.o, plan.i_at(e))
        )

    def start(self, p, value):
        plan = self.plan
        self.out[plan.row(plan.o, plan.i) * self.per + p] = value
        for d in range(1, plan.outer):
            self.first_copy(p, d).start()
        for e in range(1, plan.inner):
            self.second_copy(p, 0, e).start()

    def forward(self, p):
        plan = self.plan
        for d in range(1, plan.outer):
            self.first_copy(p, d).wait_recv()
            for e in range(1, plan.inner):
                self.second_copy(p, d, e).start()

    def finish(self):
        plan = self.plan
        for p in range(self.per):
            for d in range(1, plan.outer):
                self.first_copy(p, d).wait_send()
            for d in range(plan.outer):
                for e in range(1, plan.inner):
                    copy = self.second_copy(p, d, e)
                    copy.wait_recv()
                    copy.wait_send()


def sum_kernel(owners, per, x, out, *scratch):
    plan = Plan(owners)
    plan.barrier()
    scatter = SumScatter(plan, per, x, *scratch[:3], scratch[3:7])
    gather = Gather(plan, per, out, scratch[7:])
    scatter.start()
    for p in range(per):
        scatter.forward(p)
    for p in range(per):
        gather.start(p, scatter.total(p).astype(BF16))
    for p in range(per):
        gather.forward(p)
    scatter.finish()
    gather.finish()


def vmem():
    return pl.BlockSpec(memory_space=pltpu.VMEM)


def all_sum(x, owners, collective_id):
    per = x.shape[0] // owners
    return pl.pallas_call(
        functools.partial(sum_kernel, owners, per),
        out_shape=jax.ShapeDtypeStruct(x.shape, x.dtype),
        in_specs=[vmem()],
        out_specs=vmem(),
        scratch_shapes=SumScatter.scratch(owners, per, x.shape[1:]) + Gather.scratch(owners, per),
        compiler_params=pltpu.CompilerParams(
            collective_id=collective_id, has_side_effects=True, vmem_limit_bytes=20 << 20
        ),
        name="proj_sum",
    )(x)


def unpack_upper(packed, width):
    count = width // TILE
    tiles = {}
    offset = 0
    for i in range(count):
        for j in range(i, count):
            tile = packed[:, offset : offset + TILE]
            tiles[i, j] = tile
            if j > i:
                tiles[j, i] = tile.T
            offset += TILE
    return jnp.concatenate(
        [jnp.concatenate([tiles[i, j] for j in range(count)], axis=1) for i in range(count)], axis=0
    )


def pack_upper(full):
    width = full.shape[-1]
    return jnp.concatenate([full[at : at + TILE, at:] for at in range(0, width, TILE)], axis=1)


def mm(a, b):
    return jnp.dot(a.astype(BF16), b.astype(BF16), preferred_element_type=F32)


def factors(gram):
    width = gram.shape[-1]
    rows = lax.broadcasted_iota(jnp.int32, (width, width), 0)
    columns = lax.broadcasted_iota(jnp.int32, (width, width), 1)
    diagonal = rows == columns
    first_eye = jnp.where(diagonal, coef_first, 0.0)
    squares = jnp.sum(jnp.where(diagonal, gram, 0.0), axis=0, keepdims=True)
    total = jnp.sum(squares, axis=1, keepdims=True)
    inverse = 1.0 / (jnp.sqrt(total) + epsilon)
    a = gram * inverse * inverse
    q = None
    for sweep in range(ITERS):
        poly = coef_second * a + coef_third * mm(a, a)
        q = first_eye + poly if q is None else coef_first * q + mm(q, poly)
        if sweep < ITERS - 1:
            half = coef_first * a + mm(a, poly)
            a = coef_first * half + mm(poly, half)
    return q * inverse


def gram_kernel(owners, per, width, x, out, *scratch):
    plan = Plan(owners)
    plan.barrier()
    scatter = SumScatter(plan, per, x, *scratch[:3], scratch[3:7])
    gather = Gather(plan, per, out, scratch[7:])
    scatter.start()
    for p in range(per):
        scatter.forward(p)
    for p in range(per):
        gather.start(p, pack_upper(factors(unpack_upper(scatter.total(p), width)).astype(BF16)))
    for p in range(per):
        gather.forward(p)
    scatter.finish()
    gather.finish()


def gram_factors(x, owners, width, collective_id):
    per = x.shape[0] // owners
    return pl.pallas_call(
        functools.partial(gram_kernel, owners, per, width),
        out_shape=jax.ShapeDtypeStruct(x.shape, x.dtype),
        in_specs=[vmem()],
        out_specs=vmem(),
        scratch_shapes=SumScatter.scratch(owners, per, x.shape[1:]) + Gather.scratch(owners, per),
        compiler_params=pltpu.CompilerParams(
            collective_id=collective_id, has_side_effects=True, vmem_limit_bytes=50 << 20
        ),
        name="gram_factors",
    )(x)


def momentum_kernel(count, chosen, flags, bank, grad, basis, proj, new_bank, mom, gram):
    step = pl.program_id(0)

    @pl.when(step < count)
    def _():
        low = lax.dot_general(
            basis[0].astype(BF16), proj[0], (((0,), (0,)), ((), ())), preferred_element_type=F32
        )
        flag = residual_weight * flags[jnp.minimum(step, count - 1)].astype(F32)
        fresh = (
            momentum_decay * bank[0].astype(F32) + low + flag * (grad[0].astype(F32) - low)
        ).astype(BF16)
        new_bank[0] = fresh
        mom[0] = fresh
        width = fresh.shape[1]
        offset = 0
        for at in range(0, width, TILE):
            block = lax.dot_general(
                fresh[:, at : at + TILE],
                fresh[:, at:],
                (((0,), (0,)), ((), ())),
                preferred_element_type=F32,
            )
            gram[0, :, offset : offset + width - at] = block.astype(BF16)
            offset += width - at

    @pl.when(step >= count)
    def _():
        new_bank[0] = bank[0]


def momentum(order, refresh, bank, grads, basis_t, proj):
    count, rows, width = grads.shape
    tiles = width // TILE
    packed = TILE * (tiles * (tiles + 1) // 2)
    rank = basis_t.shape[1]

    def by_expert(step, chosen, flags):
        return (chosen[step], 0, 0)

    def by_sample(step, chosen, flags):
        return (jnp.minimum(step, count - 1), 0, 0)

    return pl.pallas_call(
        functools.partial(momentum_kernel, count),
        out_shape=(
            jax.ShapeDtypeStruct(bank.shape, bank.dtype),
            jax.ShapeDtypeStruct(grads.shape, BF16),
            jax.ShapeDtypeStruct((count, TILE, packed), BF16),
        ),
        grid_spec=pltpu.PrefetchScalarGridSpec(
            num_scalar_prefetch=2,
            grid=(bank.shape[0],),
            in_specs=[
                pl.BlockSpec((1, rows, width), by_expert),
                pl.BlockSpec((1, rows, width), by_sample),
                pl.BlockSpec((1, rank, rows), by_sample),
                pl.BlockSpec((1, rank, width), by_sample),
            ],
            out_specs=[
                pl.BlockSpec((1, rows, width), by_expert),
                pl.BlockSpec((1, rows, width), by_sample),
                pl.BlockSpec((1, TILE, packed), by_sample),
            ],
        ),
        compiler_params=pltpu.CompilerParams(dimension_semantics=("arbitrary",)),
        name="momentum",
    )(order, refresh, bank, grads, basis_t, proj)


def weights_kernel(weights, mom, packed, out):
    scale_step = step_rate * 0.2 * math.sqrt(max(D, FF))
    full = unpack_upper(packed[0], mom.shape[2])
    ortho = jnp.dot(mom[0], full, preferred_element_type=F32)
    kept = weights[0].astype(F32) * (1.0 - step_rate * decay_rate)
    out[0] = (kept - scale_step * ortho).astype(BF16)


def update_weights(weights, mom, packed):
    def block(array):
        return pl.BlockSpec((1,) + array.shape[1:], lambda step: (step, 0, 0))

    return pl.pallas_call(
        weights_kernel,
        out_shape=jax.ShapeDtypeStruct(weights.shape, weights.dtype),
        grid=(weights.shape[0],),
        in_specs=[block(weights), block(mom), block(packed)],
        out_specs=block(weights),
        compiler_params=pltpu.CompilerParams(dimension_semantics=("arbitrary",)),
        name="update_weights",
    )(weights, mom, packed)


def shards(owners, sampled, refresh, momentum_bank, weights, grads, basis):
    width = weights.shape[2]
    basis_t = jnp.swapaxes(basis, 1, 2)
    partial_sum = jnp.einsum(
        "skr,srf->skf", basis_t.astype(BF16), grads, preferred_element_type=F32
    )
    proj = all_sum(partial_sum.astype(BF16), owners, 0)
    new_bank, mom, gram = momentum(sampled[0], refresh, momentum_bank, grads, basis_t, proj)
    packed = gram_factors(gram, owners, width, 1)
    return new_bank, update_weights(weights, mom, packed)


def solution(mesh):
    in_specs = (
        P("expert", None),
        P("expert"),
        P("expert", "row", None),
        P("expert", "row", None),
        P("expert", "row", None),
        P("expert", "row", None),
    )
    out_specs = (P("expert", "row", None), P("expert", "row", None))
    return jax.shard_map(
        functools.partial(shards, mesh.shape["row"]),
        mesh=mesh,
        in_specs=in_specs,
        out_specs=out_specs,
        check_vma=False,
    )
```

```python
import functools
import math

import jax
import jax.numpy as jnp
from jax import lax
from jax.experimental import pallas as pl
from jax.experimental.pallas import tpu as pltpu
from jax.sharding import PartitionSpec as P

D = 2048
FF = 512
ITERS = 3


momentum_decay = 0.9
residual_weight = 2.0
step_rate = 0.5
decay_rate = 0.1
coef_first = 3.4445
coef_second = -4.775
coef_third = 2.0315
epsilon = 1e-07
TILE = 128
GRANT = 34 << 20
MESH = pl.DeviceIdType.MESH
F32 = jnp.float32
BF16 = jnp.bfloat16


def grid_of(owners):
    inner = 2 if owners % 2 == 0 and owners <= 8 else 4
    return owners // inner, inner


class Plan:
    def __init__(self, owners):
        self.outer, self.inner = grid_of(owners)
        me = lax.axis_index("row")
        self.o = me // self.inner
        self.i = lax.rem(me, self.inner)

    def o_at(self, d):
        return lax.rem(self.o + d, self.outer)

    def i_at(self, d):
        return lax.rem(self.i + d, self.inner)

    def row(self, o, i):
        return o * self.inner + i

    def barrier(self):
        sem = pltpu.get_barrier_semaphore()
        for d in range(1, self.inner):
            pl.semaphore_signal(
                sem, inc=1, device_id={"row": self.row(self.o, self.i_at(d))}, device_id_type=MESH
            )
        for d in range(1, self.outer):
            pl.semaphore_signal(
                sem, inc=1, device_id={"row": self.row(self.o_at(d), self.i)}, device_id_type=MESH
            )
        pl.semaphore_wait(sem, self.inner + self.outer - 2)


def remote(src, dst, send, recv, target):
    return pltpu.make_async_remote_copy(
        src_ref=src,
        dst_ref=dst,
        send_sem=send,
        recv_sem=recv,
        device_id={"row": target},
        device_id_type=MESH,
    )


class SumScatter:
    def __init__(self, plan, per, x, near, far, sums, sems):
        self.plan, self.per, self.x, self.near, self.far, self.sums = plan, per, x, near, far, sums
        self.s1, self.r1, self.s2, self.r2 = sems
        self.second = {}

    @staticmethod
    def scratch(owners, per, tile):
        outer, inner = grid_of(owners)
        dma = pltpu.SemaphoreType.DMA
        return [
            pltpu.VMEM((inner - 1, outer, per) + tile, BF16),
            pltpu.VMEM((outer - 1, per) + tile, BF16),
            pltpu.VMEM((outer, per) + tile, BF16),
            dma((inner - 1, outer, per)),
            dma((inner - 1, outer, per)),
            dma((outer - 1, per)),
            dma((outer - 1, per)),
        ]

    def steps(self):
        return [(p, d) for p in range(self.per) for d in list(range(1, self.plan.outer)) + [0]]

    def first_copy(self, p, d, e):
        plan = self.plan
        target = plan.row(plan.o, plan.i_at(e))
        return remote(
            self.x.at[plan.row(plan.o_at(d), plan.i_at(e)) * self.per + p],
            self.near.at[e - 1, d, p],
            self.s1.at[e - 1, d, p],
            self.r1.at[e - 1, d, p],
            target,
        )

    def start(self):
        for p, d in self.steps():
            for e in range(1, self.plan.inner):
                self.first_copy(p, d, e).start()

    def partial(self, p, d):
        plan = self.plan
        total = self.x[plan.row(plan.o_at(d), plan.i) * self.per + p].astype(F32)
        for e in range(1, plan.inner):
            self.first_copy(p, d, e).wait_recv()
            total = total + self.near[e - 1, d, p].astype(F32)
        return total

    def second_copy(self, p, d):
        plan = self.plan
        return remote(
            self.sums.at[d, p],
            self.far.at[d - 1, p],
            self.s2.at[d - 1, p],
            self.r2.at[d - 1, p],
            plan.row(plan.o_at(d), plan.i),
        )

    def forward_one(self, p, d):
        self.sums[d, p] = self.partial(p, d).astype(BF16)
        if d:
            self.second_copy(p, d).start()

    def forward(self, p):
        for q, d in self.steps():
            if q == p:
                self.forward_one(p, d)

    def total(self, p):
        value = self.sums[0, p].astype(F32)
        for d in range(1, self.plan.outer):
            self.second_copy(p, d).wait_recv()
            value = value + self.far[d - 1, p].astype(F32)
        return value

    def finish(self):
        for p, d in self.steps():
            for e in range(1, self.plan.inner):
                self.first_copy(p, d, e).wait_send()
            if d:
                self.second_copy(p, d).wait_send()


class Gather:
    def __init__(self, plan, per, out, sems):
        self.plan, self.per, self.out = plan, per, out
        self.s1, self.r1, self.s2, self.r2 = sems

    @staticmethod
    def scratch(owners, per):
        outer, inner = grid_of(owners)
        dma = pltpu.SemaphoreType.DMA
        return [
            dma((outer - 1, per)),
            dma((outer - 1, per)),
            dma((inner - 1, outer, per)),
            dma((inner - 1, outer, per)),
        ]

    def place(self, o, p):
        return self.out.at[self.plan.row(o, self.plan.i) * self.per + p]

    def first_copy(self, p, d):
        plan = self.plan
        own = self.place(plan.o, p)
        return remote(own, own, self.s1.at[d - 1, p], self.r1.at[d - 1, p], plan.row(plan.o_at(d), plan.i))

    def second_copy(self, p, d, e):
        plan = self.plan
        own = self.place(plan.o_at(plan.outer - d), p)
        return remote(
            own, own, self.s2.at[e - 1, d, p], self.r2.at[e - 1, d, p], plan.row(plan.o, plan.i_at(e))
        )

    def mine(self, p):
        return self.plan.row(self.plan.o, self.plan.i) * self.per + p

    def start(self, p):
        plan = self.plan
        for d in range(1, plan.outer):
            self.first_copy(p, d).start()
        for e in range(1, plan.inner):
            self.second_copy(p, 0, e).start()

    def forward(self, p):
        plan = self.plan
        for d in range(1, plan.outer):
            self.first_copy(p, d).wait_recv()
            for e in range(1, plan.inner):
                self.second_copy(p, d, e).start()

    def arrive(self, p, d):
        plan = self.plan
        places = []
        for e in range(1, plan.inner):
            self.second_copy(p, d, e).wait_recv()
            places.append(plan.row(plan.o_at(plan.outer - d), plan.i_at(plan.inner - e)) * self.per + p)
        return places

    def finish(self):
        plan = self.plan
        for p in range(self.per):
            for d in range(1, plan.outer):
                self.first_copy(p, d).wait_send()
            for d in range(plan.outer):
                for e in range(1, plan.inner):
                    self.second_copy(p, d, e).wait_send()


def sum_kernel(owners, per, x, out, *scratch):
    plan = Plan(owners)
    plan.barrier()
    scatter = SumScatter(plan, per, x, *scratch[:3], scratch[3:7])
    gather = Gather(plan, per, out, scratch[7:])
    scatter.start()
    for p in range(per):
        scatter.forward(p)
    for p in range(per):
        out[gather.mine(p)] = scatter.total(p).astype(BF16)
        gather.start(p)
    for p in range(per):
        gather.forward(p)
    for p in range(per):
        for d in range(plan.outer):
            gather.arrive(p, d)
    scatter.finish()
    gather.finish()


def vmem():
    return pl.BlockSpec(memory_space=pltpu.VMEM)


def all_sum(x, owners, collective_id):
    per = x.shape[0] // owners
    return pl.pallas_call(
        functools.partial(sum_kernel, owners, per),
        out_shape=jax.ShapeDtypeStruct(x.shape, x.dtype),
        in_specs=[vmem()],
        out_specs=vmem(),
        scratch_shapes=SumScatter.scratch(owners, per, x.shape[1:]) + Gather.scratch(owners, per),
        compiler_params=pltpu.CompilerParams(
            collective_id=collective_id, has_side_effects=True, vmem_limit_bytes=20 << 20
        ),
        name="proj_sum",
    )(x)


def triangle():
    rows = lax.broadcasted_iota(jnp.int32, (TILE, TILE), 0)
    columns = lax.broadcasted_iota(jnp.int32, (TILE, TILE), 1)
    return rows, columns


def pairs(count):
    return [(i, j) for i in range(count) for j in range(i + 1, count)]


EXTRA = 16


def packed_rows(width):
    count = width // TILE
    return TILE * (len(pairs(count)) + count // 2) + EXTRA


def pack(tile):
    count = tile.count
    rows, columns = triangle()
    at = 0
    for i, j in pairs(count):
        yield at, tile(i, j).astype(BF16)
        at += TILE
    extra = lax.broadcasted_iota(jnp.int32, (EXTRA, TILE), 0)
    diagonals = jnp.zeros((EXTRA, TILE), F32)
    for k in range(0, count, 2):
        upper, lower = tile(k, k), tile(k + 1, k + 1)
        yield at, jnp.where(rows <= columns, upper, lower).astype(BF16)
        at += TILE
        diagonal = jnp.sum(jnp.where(rows == columns, lower, 0.0), axis=0, keepdims=True)
        diagonals = jnp.where(extra == k // 2, diagonal, diagonals)
    yield at, diagonals.astype(BF16)


class Tiles:
    def __init__(self, count, get):
        self.count, self.get = count, get

    def __call__(self, i, j):
        return self.get(i, j)


def unpack(packed, width, dtype):
    count = width // TILE
    rows, columns = triangle()
    tiles = {}
    at = 0
    for i, j in pairs(count):
        tile = packed[at : at + TILE].astype(dtype)
        tiles[i, j], tiles[j, i] = tile, tile.T
        at += TILE
    diagonals = packed[at + TILE * (count // 2) :].astype(F32)
    for k in range(0, count, 2):
        both = packed[at : at + TILE].astype(F32)
        other = both.T
        line = diagonals[k // 2 : k // 2 + 1]
        tiles[k, k] = jnp.where(rows <= columns, both, other).astype(dtype)
        lower = jnp.where(rows > columns, both, other)
        tiles[k + 1, k + 1] = jnp.where(rows == columns, line, lower).astype(dtype)
        at += TILE
    return jnp.concatenate(
        [jnp.concatenate([tiles[i, j] for j in range(count)], axis=1) for i in range(count)], axis=0
    )


def mm(a, b):
    return jnp.dot(a.astype(BF16), b.astype(BF16), preferred_element_type=F32)


def factors(gram):
    width = gram.shape[-1]
    rows = lax.broadcasted_iota(jnp.int32, (width, width), 0)
    columns = lax.broadcasted_iota(jnp.int32, (width, width), 1)
    diagonal = rows == columns
    first_eye = jnp.where(diagonal, coef_first, 0.0)
    squares = jnp.sum(jnp.where(diagonal, gram, 0.0), axis=0, keepdims=True)
    total = jnp.sum(squares, axis=1, keepdims=True)
    inverse = 1.0 / (jnp.sqrt(total) + epsilon)
    a = gram * inverse * inverse
    q = None
    for sweep in range(ITERS):
        poly = coef_second * a + coef_third * mm(a, a)
        q = first_eye + poly if q is None else coef_first * q + mm(q, poly)
        if sweep < ITERS - 1:
            half = coef_first * a + mm(a, poly)
            a = coef_first * half + mm(poly, half)
    return q * inverse


def store_gram(mom, s, x):
    fresh = mom[s]
    width = fresh.shape[1]
    lines = {}

    def tile(i, j):
        if i not in lines:
            lines[i] = lax.dot_general(
                fresh[:, i * TILE : (i + 1) * TILE],
                fresh[:, i * TILE :],
                (((0,), (0,)), ((), ())),
                preferred_element_type=F32,
            )
        return lines[i][:, (j - i) * TILE : (j - i + 1) * TILE]

    for at, piece in pack(Tiles(width // TILE, tile)):
        x[s, at : at + piece.shape[0]] = piece


def store_factors(value, width, s, out):
    q = factors(unpack(value, width, F32))

    def tile(i, j):
        return q[i * TILE : (i + 1) * TILE, j * TILE : (j + 1) * TILE]

    for at, piece in pack(Tiles(width // TILE, tile)):
        out[s, at : at + piece.shape[0]] = piece


def store_weights(weights, mom, packed, s, out):
    scale_step = step_rate * 0.2 * math.sqrt(max(D, FF))
    full = unpack(packed[s], mom.shape[2], BF16)
    ortho = jnp.dot(mom[s], full, preferred_element_type=F32)
    kept = weights[s].astype(F32) * (1.0 - step_rate * decay_rate)
    out[s] = (kept - scale_step * ortho).astype(BF16)


def gram_kernel(owners, per, mom, weights, out, x, packed, *scratch):
    width = mom.shape[2]
    plan = Plan(owners)
    plan.barrier()
    scatter = SumScatter(plan, per, x, *scratch[:3], scratch[3:7])
    gather = Gather(plan, per, packed, scratch[7:])
    outer, inner = plan.outer, plan.inner

    def first(p):
        @pl.loop(1, outer + 1)
        def _(later):
            d = lax.rem(later, outer)
            for e in range(1, inner):
                store_gram(mom, plan.row(plan.o_at(d), plan.i_at(e)) * per + p, x)
                scatter.first_copy(p, d, e).start()

    def own(p):
        @pl.loop(0, outer)
        def _(d):
            store_gram(mom, plan.row(plan.o_at(d), plan.i) * per + p, x)

    def owner_work(p):
        store_factors(scatter.total(p), width, gather.mine(p), packed)
        gather.start(p)

    def last(p):
        for d in range(outer):
            store_weights(weights, mom, packed, plan.row(plan.o_at(outer - d), plan.i) * per + p, out)
            for s in gather.arrive(p, d):
                store_weights(weights, mom, packed, s, out)

    for p in range(per):
        first(p)
        own(p)
    scatter.forward(0)
    for p in range(per):
        if p + 1 < per:
            scatter.forward_one(p + 1, 1)
        owner_work(p)
        if p + 1 < per:
            for d in list(range(2, outer)) + [0]:
                scatter.forward_one(p + 1, d)
            gather.forward(p)
    gather.forward(per - 1)
    for p in range(per):
        last(p)
    scatter.finish()
    gather.finish()


def gram_update(mom, weights, owners, collective_id):
    count, rows, width = mom.shape
    per = count // owners
    tile = (packed_rows(width), TILE)
    return pl.pallas_call(
        functools.partial(gram_kernel, owners, per),
        out_shape=jax.ShapeDtypeStruct(weights.shape, weights.dtype),
        in_specs=[vmem(), vmem()],
        out_specs=vmem(),
        scratch_shapes=[pltpu.VMEM((count,) + tile, BF16), pltpu.VMEM((count,) + tile, BF16)]
        + SumScatter.scratch(owners, per, tile)
        + Gather.scratch(owners, per),
        compiler_params=pltpu.CompilerParams(
            collective_id=collective_id, has_side_effects=True, vmem_limit_bytes=GRANT
        ),
        name="gram_update",
    )(mom, weights)


def momentum_kernel(count, chosen, flags, bank, grad, basis, proj, new_bank, mom):
    step = pl.program_id(0)

    @pl.when(step < count)
    def _():
        low = lax.dot_general(
            basis[0].astype(BF16), proj[0], (((0,), (0,)), ((), ())), preferred_element_type=F32
        )
        flag = residual_weight * flags[jnp.minimum(step, count - 1)].astype(F32)
        fresh = (
            momentum_decay * bank[0].astype(F32) + low + flag * (grad[0].astype(F32) - low)
        ).astype(BF16)
        new_bank[0] = fresh
        mom[0] = fresh

    @pl.when(step >= count)
    def _():
        new_bank[0] = bank[0]


def momentum(order, refresh, bank, grads, basis_t, proj):
    count, rows, width = grads.shape
    rank = basis_t.shape[1]

    def by_expert(step, chosen, flags):
        return (chosen[step], 0, 0)

    def by_sample(step, chosen, flags):
        return (jnp.minimum(step, count - 1), 0, 0)

    return pl.pallas_call(
        functools.partial(momentum_kernel, count),
        out_shape=(
            jax.ShapeDtypeStruct(bank.shape, bank.dtype),
            jax.ShapeDtypeStruct(grads.shape, BF16),
        ),
        grid_spec=pltpu.PrefetchScalarGridSpec(
            num_scalar_prefetch=2,
            grid=(bank.shape[0],),
            in_specs=[
                pl.BlockSpec((1, rows, width), by_expert),
                pl.BlockSpec((1, rows, width), by_sample),
                pl.BlockSpec((1, rank, rows), by_sample),
                pl.BlockSpec((1, rank, width), by_sample),
            ],
            out_specs=[
                pl.BlockSpec((1, rows, width), by_expert),
                pl.BlockSpec((1, rows, width), by_sample),
            ],
        ),
        compiler_params=pltpu.CompilerParams(dimension_semantics=("arbitrary",)),
        name="momentum",
    )(order, refresh, bank, grads, basis_t, proj)


def shards(owners, sampled, refresh, momentum_bank, weights, grads, basis):
    basis_t = jnp.swapaxes(basis, 1, 2)
    partial_sum = jnp.einsum(
        "skr,srf->skf", basis_t.astype(BF16), grads, preferred_element_type=F32
    )
    proj = all_sum(partial_sum.astype(BF16), owners, 0)
    new_bank, mom = momentum(sampled[0], refresh, momentum_bank, grads, basis_t, proj)
    return new_bank, gram_update(mom, weights, owners, 1)


def solution(mesh):
    in_specs = (
        P("expert", None),
        P("expert"),
        P("expert", "row", None),
        P("expert", "row", None),
        P("expert", "row", None),
        P("expert", "row", None),
    )
    out_specs = (P("expert", "row", None), P("expert", "row", None))
    return jax.shard_map(
        functools.partial(shards, mesh.shape["row"]),
        mesh=mesh,
        in_specs=in_specs,
        out_specs=out_specs,
        check_vma=False,
    )
```

```python
import functools
import math

import jax
import jax.numpy as jnp
from jax import lax
from jax.experimental import pallas as pl
from jax.experimental.pallas import tpu as pltpu
from jax.sharding import PartitionSpec as P

D = 2048
FF = 512
ITERS = 3


momentum_decay = 0.9
residual_weight = 2.0
step_rate = 0.5
decay_rate = 0.1
coef_first = 3.4445
coef_second = -4.775
coef_third = 2.0315
epsilon = 1e-07
TILE = 128
SPARE = 21 << 20
MESH = pl.DeviceIdType.MESH
F32 = jnp.float32
BF16 = jnp.bfloat16


def grid_of(owners):
    inner = 2 if owners % 2 == 0 and owners <= 8 else 4
    return owners // inner, inner


class Plan:
    def __init__(self, owners):
        self.outer, self.inner = grid_of(owners)
        me = lax.axis_index("row")
        self.o = me // self.inner
        self.i = lax.rem(me, self.inner)

    def o_at(self, d):
        return lax.rem(self.o + d, self.outer)

    def i_at(self, d):
        return lax.rem(self.i + d, self.inner)

    def row(self, o, i):
        return o * self.inner + i

    def barrier(self):
        sem = pltpu.get_barrier_semaphore()
        for d in range(1, self.inner):
            pl.semaphore_signal(
                sem, inc=1, device_id={"row": self.row(self.o, self.i_at(d))}, device_id_type=MESH
            )
        for d in range(1, self.outer):
            pl.semaphore_signal(
                sem, inc=1, device_id={"row": self.row(self.o_at(d), self.i)}, device_id_type=MESH
            )
        pl.semaphore_wait(sem, self.inner + self.outer - 2)


def remote(src, dst, send, recv, target):
    return pltpu.make_async_remote_copy(
        src_ref=src,
        dst_ref=dst,
        send_sem=send,
        recv_sem=recv,
        device_id={"row": target},
        device_id_type=MESH,
    )


class SumScatter:
    def __init__(self, plan, per, x, near, far, sems):
        self.plan, self.per, self.x, self.near, self.far = plan, per, x, near, far
        self.s1, self.r1, self.s2, self.r2 = sems

    @staticmethod
    def scratch(owners, per, tile):
        outer, inner = grid_of(owners)
        dma = pltpu.SemaphoreType.DMA
        return [
            pltpu.VMEM((inner - 1, outer, per) + tile, BF16),
            pltpu.VMEM((outer - 1, per) + tile, BF16),
            dma((inner - 1, outer, per)),
            dma((inner - 1, outer, per)),
            dma((outer - 1, per)),
            dma((outer - 1, per)),
        ]

    def steps(self):
        return [(p, d) for p in range(self.per) for d in list(range(1, self.plan.outer)) + [0]]

    def first_copy(self, p, d, e):
        plan = self.plan
        target = plan.row(plan.o, plan.i_at(e))
        return remote(
            self.x.at[plan.row(plan.o_at(d), plan.i_at(e)) * self.per + p],
            self.near.at[e - 1, d, p],
            self.s1.at[e - 1, d, p],
            self.r1.at[e - 1, d, p],
            target,
        )

    def start(self):
        for p, d in self.steps():
            for e in range(1, self.plan.inner):
                self.first_copy(p, d, e).start()

    def column(self, p, d):
        return self.plan.row(self.plan.o_at(d), self.plan.i) * self.per + p

    def partial(self, p, d):
        plan = self.plan
        total = self.x[self.column(p, d)].astype(F32)
        for e in range(1, plan.inner):
            self.first_copy(p, d, e).wait_recv()
            total = total + self.near[e - 1, d, p].astype(F32)
        return total

    def second_copy(self, p, d):
        plan = self.plan
        return remote(
            self.x.at[self.column(p, d)],
            self.far.at[d - 1, p],
            self.s2.at[d - 1, p],
            self.r2.at[d - 1, p],
            plan.row(plan.o_at(d), plan.i),
        )

    def forward_one(self, p, d):
        self.x[self.column(p, d)] = self.partial(p, d).astype(BF16)
        if d:
            self.second_copy(p, d).start()

    def forward(self, p):
        for q, d in self.steps():
            if q == p:
                self.forward_one(p, d)

    def total(self, p):
        value = self.x[self.column(p, 0)].astype(F32)
        for d in range(1, self.plan.outer):
            self.second_copy(p, d).wait_recv()
            value = value + self.far[d - 1, p].astype(F32)
        return value

    def finish(self):
        for p, d in self.steps():
            for e in range(1, self.plan.inner):
                self.first_copy(p, d, e).wait_send()
            if d:
                self.second_copy(p, d).wait_send()


class Gather:
    def __init__(self, plan, per, out, sems):
        self.plan, self.per, self.out = plan, per, out
        self.s1, self.r1, self.s2, self.r2 = sems

    @staticmethod
    def scratch(owners, per):
        outer, inner = grid_of(owners)
        dma = pltpu.SemaphoreType.DMA
        return [
            dma((outer - 1, per)),
            dma((outer - 1, per)),
            dma((inner - 1, outer, per)),
            dma((inner - 1, outer, per)),
        ]

    def place(self, o, p):
        return self.out.at[self.plan.row(o, self.plan.i) * self.per + p]

    def first_copy(self, p, d):
        plan = self.plan
        own = self.place(plan.o, p)
        return remote(own, own, self.s1.at[d - 1, p], self.r1.at[d - 1, p], plan.row(plan.o_at(d), plan.i))

    def second_copy(self, p, d, e):
        plan = self.plan
        own = self.place(plan.o_at(plan.outer - d), p)
        return remote(
            own, own, self.s2.at[e - 1, d, p], self.r2.at[e - 1, d, p], plan.row(plan.o, plan.i_at(e))
        )

    def mine(self, p):
        return self.plan.row(self.plan.o, self.plan.i) * self.per + p

    def start(self, p):
        plan = self.plan
        for d in range(1, plan.outer):
            self.first_copy(p, d).start()
        for e in range(1, plan.inner):
            self.second_copy(p, 0, e).start()

    def forward(self, p):
        plan = self.plan
        for d in range(1, plan.outer):
            self.first_copy(p, d).wait_recv()
            for e in range(1, plan.inner):
                self.second_copy(p, d, e).start()

    def arrive(self, p, d):
        plan = self.plan
        places = []
        for e in range(1, plan.inner):
            self.second_copy(p, d, e).wait_recv()
            places.append(plan.row(plan.o_at(plan.outer - d), plan.i_at(plan.inner - e)) * self.per + p)
        return places

    def finish(self):
        plan = self.plan
        for p in range(self.per):
            for d in range(1, plan.outer):
                self.first_copy(p, d).wait_send()
            for d in range(plan.outer):
                for e in range(1, plan.inner):
                    self.second_copy(p, d, e).wait_send()


def vmem():
    return pl.BlockSpec(memory_space=pltpu.VMEM)


def triangle():
    rows = lax.broadcasted_iota(jnp.int32, (TILE, TILE), 0)
    columns = lax.broadcasted_iota(jnp.int32, (TILE, TILE), 1)
    return rows, columns


def pairs(count):
    return [(i, j) for i in range(count) for j in range(i + 1, count)]


EXTRA = 16


def packed_rows(width):
    count = width // TILE
    return TILE * (len(pairs(count)) + count // 2) + EXTRA


def pack(tile):
    count = tile.count
    rows, columns = triangle()
    at = 0
    for i, j in pairs(count):
        yield at, tile(i, j).astype(BF16)
        at += TILE
    extra = lax.broadcasted_iota(jnp.int32, (EXTRA, TILE), 0)
    diagonals = jnp.zeros((EXTRA, TILE), F32)
    for k in range(0, count, 2):
        upper, lower = tile(k, k), tile(k + 1, k + 1)
        yield at, jnp.where(rows <= columns, upper, lower).astype(BF16)
        at += TILE
        diagonal = jnp.sum(jnp.where(rows == columns, lower, 0.0), axis=0, keepdims=True)
        diagonals = jnp.where(extra == k // 2, diagonal, diagonals)
    yield at, diagonals.astype(BF16)


class Tiles:
    def __init__(self, count, get):
        self.count, self.get = count, get

    def __call__(self, i, j):
        return self.get(i, j)


def unpack(packed, width, dtype):
    count = width // TILE
    rows, columns = triangle()
    tiles = {}
    at = 0
    for i, j in pairs(count):
        tile = packed[at : at + TILE].astype(dtype)
        tiles[i, j], tiles[j, i] = tile, tile.T
        at += TILE
    diagonals = packed[at + TILE * (count // 2) :].astype(F32)
    for k in range(0, count, 2):
        both = packed[at : at + TILE].astype(F32)
        other = both.T
        line = diagonals[k // 2 : k // 2 + 1]
        tiles[k, k] = jnp.where(rows <= columns, both, other).astype(dtype)
        lower = jnp.where(rows > columns, both, other)
        tiles[k + 1, k + 1] = jnp.where(rows == columns, line, lower).astype(dtype)
        at += TILE
    return jnp.concatenate(
        [jnp.concatenate([tiles[i, j] for j in range(count)], axis=1) for i in range(count)], axis=0
    )


def mm(a, b):
    return jnp.dot(a.astype(BF16), b.astype(BF16), preferred_element_type=F32)


def factors(gram):
    width = gram.shape[-1]
    rows = lax.broadcasted_iota(jnp.int32, (width, width), 0)
    columns = lax.broadcasted_iota(jnp.int32, (width, width), 1)
    diagonal = rows == columns
    first_eye = jnp.where(diagonal, coef_first, 0.0)
    squares = jnp.sum(jnp.where(diagonal, gram, 0.0), axis=0, keepdims=True)
    total = jnp.sum(squares, axis=1, keepdims=True)
    inverse = 1.0 / (jnp.sqrt(total) + epsilon)
    a = gram * inverse * inverse
    q = None
    for sweep in range(ITERS):
        poly = coef_second * a + coef_third * mm(a, a)
        q = first_eye + poly if q is None else coef_first * q + mm(q, poly)
        if sweep < ITERS - 1:
            half = coef_first * a + mm(a, poly)
            a = coef_first * half + mm(poly, half)
    return q * inverse


def store_gram(mom, s, x):
    fresh = mom[s]
    width = fresh.shape[1]
    lines = {}

    def tile(i, j):
        if i not in lines:
            lines[i] = lax.dot_general(
                fresh[:, i * TILE : (i + 1) * TILE],
                fresh[:, i * TILE :],
                (((0,), (0,)), ((), ())),
                preferred_element_type=F32,
            )
        return lines[i][:, (j - i) * TILE : (j - i + 1) * TILE]

    for at, piece in pack(Tiles(width // TILE, tile)):
        x[s, at : at + piece.shape[0]] = piece


def store_factors(value, width, s, out):
    q = factors(unpack(value, width, F32))

    def tile(i, j):
        return q[i * TILE : (i + 1) * TILE, j * TILE : (j + 1) * TILE]

    for at, piece in pack(Tiles(width // TILE, tile)):
        out[s, at : at + piece.shape[0]] = piece


def store_weights(mom, packed, s, out):
    scale_step = step_rate * 0.2 * math.sqrt(max(D, FF))
    full = unpack(packed[s], mom.shape[2], BF16)
    ortho = jnp.dot(mom[s], full, preferred_element_type=F32)
    kept = out[s].astype(F32) * (1.0 - step_rate * decay_rate)
    out[s] = (kept - scale_step * ortho).astype(BF16)


def store_projection(basis, grads, s, out):
    out[s] = jnp.dot(basis[s].astype(BF16), grads[s], preferred_element_type=F32).astype(BF16)


def store_momentum(flags, old, grads, basis, proj, s, mom):
    low = lax.dot_general(
        basis[s].astype(BF16), proj[s], (((0,), (0,)), ((), ())), preferred_element_type=F32
    )
    flag = residual_weight * flags[s].astype(F32)
    grad_full = grads[s].astype(F32)
    mom[s] = (momentum_decay * old[s].astype(F32) + low + flag * (grad_full - low)).astype(BF16)


def step_kernel(owners, per, flags, old, grads, basis, weights, mom, out, fetched, px, proj, x, packed, *scratch):
    width = mom.shape[2]
    fetch = pltpu.make_async_copy(weights, out, fetched)
    fetch.start()
    plan = Plan(owners)
    plan.barrier()
    proj_scatter = SumScatter(plan, per, px, *scratch[:2], scratch[2:6])
    proj_gather = Gather(plan, per, proj, scratch[6:10])
    scatter = SumScatter(plan, per, x, *scratch[10:12], scratch[12:16])
    gather = Gather(plan, per, packed, scratch[16:])
    outer, inner = plan.outer, plan.inner

    def project(p):
        @pl.loop(1, outer + 1)
        def _(later):
            d = lax.rem(later, outer)
            for e in range(1, inner):
                store_projection(basis, grads, plan.row(plan.o_at(d), plan.i_at(e)) * per + p, px)
                proj_scatter.first_copy(p, d, e).start()

    def project_own(p):
        @pl.loop(0, outer)
        def _(d):
            store_projection(basis, grads, plan.row(plan.o_at(d), plan.i) * per + p, px)

    def own_sum(p):
        proj[proj_gather.mine(p)] = proj_scatter.total(p).astype(BF16)
        proj_gather.start(p)

    def prepare(s):
        store_momentum(flags, old, grads, basis, proj, s, mom)
        store_gram(mom, s, x)

    def first(p):
        @pl.loop(1, outer + 1)
        def _(later):
            d = lax.rem(later, outer)
            for e in range(1, inner):
                prepare(plan.row(plan.o_at(d), plan.i_at(e)) * per + p)
                scatter.first_copy(p, d, e).start()

    def own(p):
        @pl.loop(0, outer)
        def _(d):
            prepare(plan.row(plan.o_at(d), plan.i) * per + p)

    def owner_work(p):
        store_factors(scatter.total(p), width, gather.mine(p), packed)
        gather.start(p)

    def last(p):
        for d in range(outer):
            store_weights(mom, packed, plan.row(plan.o_at(outer - d), plan.i) * per + p, out)
            for s in gather.arrive(p, d):
                store_weights(mom, packed, s, out)

    for p in range(per):
        project(p)
    for p in range(per):
        project_own(p)
    for p in range(per):
        proj_scatter.forward(p)
        if p:
            own_sum(p - 1)
    own_sum(per - 1)
    for p in range(per):
        proj_gather.forward(p)
        for d in range(outer):
            proj_gather.arrive(p, d)
        first(p)
    for p in range(per):
        own(p)
    scatter.forward(0)
    for p in range(per):
        if p + 1 < per:
            scatter.forward_one(p + 1, 1)
        owner_work(p)
        if p + 1 < per:
            for d in list(range(2, outer)) + [0]:
                scatter.forward_one(p + 1, d)
            gather.forward(p)
    gather.forward(per - 1)
    fetch.wait()
    for p in range(per):
        last(p)
    proj_scatter.finish()
    proj_gather.finish()
    scatter.finish()
    gather.finish()


def step(refresh, old, grads, basis_t, weights, owners):
    count, rows, width = grads.shape
    per = count // owners
    tile = (packed_rows(width), TILE)
    line = (basis_t.shape[1], width)
    scratch = (
        [pltpu.SemaphoreType.DMA]
        + [pltpu.VMEM((count,) + line, BF16)] * 2
        + [pltpu.VMEM((count,) + tile, BF16)] * 2
        + SumScatter.scratch(owners, per, line)
        + Gather.scratch(owners, per)
        + SumScatter.scratch(owners, per, tile)
        + Gather.scratch(owners, per)
    )
    held = sum(2 * math.prod(one.shape) for one in scratch if one.dtype == BF16)
    return pl.pallas_call(
        functools.partial(step_kernel, owners, per),
        out_shape=(
            jax.ShapeDtypeStruct(weights.shape, BF16),
            jax.ShapeDtypeStruct(weights.shape, weights.dtype),
        ),
        in_specs=[pl.BlockSpec(memory_space=pltpu.SMEM)]
        + [vmem()] * 3
        + [pl.BlockSpec(memory_space=pltpu.HBM)],
        out_specs=(vmem(), vmem()),
        scratch_shapes=scratch,
        compiler_params=pltpu.CompilerParams(
            collective_id=0, has_side_effects=True, vmem_limit_bytes=held + SPARE
        ),
        name="step",
    )(refresh, old, grads, basis_t, weights)


def take_kernel(count, order, bank, new_bank, old, stage, came, went):
    total = bank.shape[0]

    def reading(j):
        target = old.at[j] if j < count else stage.at[j - count]
        return pltpu.make_async_copy(bank.at[order[j]], target, came.at[j])

    def writing(j):
        return pltpu.make_async_copy(stage.at[j - count], new_bank.at[order[j]], went.at[j - count])

    for j in list(range(count, total)) + list(range(count)):
        reading(j).start()
    for j in range(count, total):
        reading(j).wait()
        writing(j).start()
    for j in range(count):
        reading(j).wait()
    for j in range(count, total):
        writing(j).wait()


def take(order, bank, count):
    others = max(bank.shape[0] - count, 1)
    shape = bank.shape[1:]
    return pl.pallas_call(
        functools.partial(take_kernel, count),
        out_shape=(
            jax.ShapeDtypeStruct(bank.shape, bank.dtype),
            jax.ShapeDtypeStruct((count,) + shape, bank.dtype),
        ),
        in_specs=[pl.BlockSpec(memory_space=pltpu.SMEM), pl.BlockSpec(memory_space=pltpu.HBM)],
        out_specs=(pl.BlockSpec(memory_space=pltpu.HBM), vmem()),
        scratch_shapes=[
            pltpu.VMEM((others,) + shape, bank.dtype),
            pltpu.SemaphoreType.DMA((bank.shape[0],)),
            pltpu.SemaphoreType.DMA((others,)),
        ],
        compiler_params=pltpu.CompilerParams(vmem_limit_bytes=46 << 20),
        name="take",
    )(order, bank)


def put_kernel(order, kept, mom, new_bank, sems):
    def writing(j):
        return pltpu.make_async_copy(mom.at[j], new_bank.at[order[j]], sems.at[j])

    for j in range(mom.shape[0]):
        writing(j).start()
    for j in range(mom.shape[0]):
        writing(j).wait()


def put(order, kept, mom):
    return pl.pallas_call(
        put_kernel,
        out_shape=jax.ShapeDtypeStruct(kept.shape, kept.dtype),
        in_specs=[
            pl.BlockSpec(memory_space=pltpu.SMEM),
            pl.BlockSpec(memory_space=pltpu.HBM),
            vmem(),
        ],
        out_specs=pl.BlockSpec(memory_space=pltpu.HBM),
        scratch_shapes=[pltpu.SemaphoreType.DMA((mom.shape[0],))],
        input_output_aliases={1: 0},
        compiler_params=pltpu.CompilerParams(vmem_limit_bytes=1 << 20),
        name="put",
    )(order, kept, mom)


def shards(owners, sampled, refresh, momentum_bank, weights, grads, basis):
    order = sampled[0]
    kept, old = take(order, momentum_bank, weights.shape[0])
    mom, new_weights = step(refresh, old, grads, jnp.swapaxes(basis, 1, 2), weights, owners)
    return put(order, kept, mom), new_weights


def solution(mesh):
    in_specs = (
        P("expert", None),
        P("expert"),
        P("expert", "row", None),
        P("expert", "row", None),
        P("expert", "row", None),
        P("expert", "row", None),
    )
    out_specs = (P("expert", "row", None), P("expert", "row", None))
    return jax.shard_map(
        functools.partial(shards, mesh.shape["row"]),
        mesh=mesh,
        in_specs=in_specs,
        out_specs=out_specs,
        check_vma=False,
    )
```

```python
import functools
import math

import jax
import jax.numpy as jnp
from jax import lax
from jax.experimental import pallas as pl
from jax.experimental.pallas import tpu as pltpu
from jax.sharding import PartitionSpec as P

D = 2048
FF = 512
ITERS = 3


momentum_decay = 0.9
residual_weight = 2.0
step_rate = 0.5
decay_rate = 0.1
coef_first = 3.4445
coef_second = -4.775
coef_third = 2.0315
epsilon = 1e-07
TILE = 128
SPARE = 21 << 20
MESH = pl.DeviceIdType.MESH
F32 = jnp.float32
BF16 = jnp.bfloat16


def grid_of(owners):
    inner = 2 if owners % 2 == 0 and owners <= 8 else 4
    return owners // inner, inner


class Plan:
    def __init__(self, owners):
        self.outer, self.inner = grid_of(owners)
        me = lax.axis_index("row")
        self.o = me // self.inner
        self.i = lax.rem(me, self.inner)

    def o_at(self, d):
        return lax.rem(self.o + d, self.outer)

    def i_at(self, d):
        return lax.rem(self.i + d, self.inner)

    def row(self, o, i):
        return o * self.inner + i

    def barrier(self):
        sem = pltpu.get_barrier_semaphore()
        for d in range(1, self.inner):
            pl.semaphore_signal(
                sem, inc=1, device_id={"row": self.row(self.o, self.i_at(d))}, device_id_type=MESH
            )
        for d in range(1, self.outer):
            pl.semaphore_signal(
                sem, inc=1, device_id={"row": self.row(self.o_at(d), self.i)}, device_id_type=MESH
            )
        pl.semaphore_wait(sem, self.inner + self.outer - 2)


def remote(src, dst, send, recv, target):
    return pltpu.make_async_remote_copy(
        src_ref=src,
        dst_ref=dst,
        send_sem=send,
        recv_sem=recv,
        device_id={"row": target},
        device_id_type=MESH,
    )


class SumScatter:
    def __init__(self, plan, per, x, near, far, sems):
        self.plan, self.per, self.x, self.near, self.far = plan, per, x, near, far
        self.s1, self.r1, self.s2, self.r2 = sems

    @staticmethod
    def scratch(owners, per, tile):
        outer, inner = grid_of(owners)
        dma = pltpu.SemaphoreType.DMA
        return [
            pltpu.VMEM((inner - 1, outer, per) + tile, BF16),
            pltpu.VMEM((outer - 1, per) + tile, BF16),
            dma((inner - 1, outer, per)),
            dma((inner - 1, outer, per)),
            dma((outer - 1, per)),
            dma((outer - 1, per)),
        ]

    def steps(self):
        return [(p, d) for p in range(self.per) for d in list(range(1, self.plan.outer)) + [0]]

    def first_copy(self, p, d, e):
        plan = self.plan
        target = plan.row(plan.o, plan.i_at(e))
        return remote(
            self.x.at[plan.row(plan.o_at(d), plan.i_at(e)) * self.per + p],
            self.near.at[e - 1, d, p],
            self.s1.at[e - 1, d, p],
            self.r1.at[e - 1, d, p],
            target,
        )

    def start(self):
        for p, d in self.steps():
            for e in range(1, self.plan.inner):
                self.first_copy(p, d, e).start()

    def column(self, p, d):
        return self.plan.row(self.plan.o_at(d), self.plan.i) * self.per + p

    def partial(self, p, d):
        plan = self.plan
        total = self.x[self.column(p, d)].astype(F32)
        for e in range(1, plan.inner):
            self.first_copy(p, d, e).wait_recv()
            total = total + self.near[e - 1, d, p].astype(F32)
        return total

    def second_copy(self, p, d):
        plan = self.plan
        return remote(
            self.x.at[self.column(p, d)],
            self.far.at[d - 1, p],
            self.s2.at[d - 1, p],
            self.r2.at[d - 1, p],
            plan.row(plan.o_at(d), plan.i),
        )

    def forward_one(self, p, d):
        self.x[self.column(p, d)] = self.partial(p, d).astype(BF16)
        if d:
            self.second_copy(p, d).start()

    def forward(self, p):
        for q, d in self.steps():
            if q == p:
                self.forward_one(p, d)

    def total(self, p):
        value = self.x[self.column(p, 0)].astype(F32)
        for d in range(1, self.plan.outer):
            self.second_copy(p, d).wait_recv()
            value = value + self.far[d - 1, p].astype(F32)
        return value

    def finish(self):
        for p, d in self.steps():
            for e in range(1, self.plan.inner):
                self.first_copy(p, d, e).wait_send()
            if d:
                self.second_copy(p, d).wait_send()


class Gather:
    def __init__(self, plan, per, out, sems):
        self.plan, self.per, self.out = plan, per, out
        self.s1, self.r1, self.s2, self.r2 = sems

    @staticmethod
    def scratch(owners, per):
        outer, inner = grid_of(owners)
        dma = pltpu.SemaphoreType.DMA
        return [
            dma((outer - 1, per)),
            dma((outer - 1, per)),
            dma((inner - 1, outer, per)),
            dma((inner - 1, outer, per)),
        ]

    def place(self, o, p):
        return self.out.at[self.plan.row(o, self.plan.i) * self.per + p]

    def first_copy(self, p, d):
        plan = self.plan
        own = self.place(plan.o, p)
        return remote(own, own, self.s1.at[d - 1, p], self.r1.at[d - 1, p], plan.row(plan.o_at(d), plan.i))

    def second_copy(self, p, d, e):
        plan = self.plan
        own = self.place(plan.o_at(plan.outer - d), p)
        return remote(
            own, own, self.s2.at[e - 1, d, p], self.r2.at[e - 1, d, p], plan.row(plan.o, plan.i_at(e))
        )

    def mine(self, p):
        return self.plan.row(self.plan.o, self.plan.i) * self.per + p

    def start(self, p):
        plan = self.plan
        for d in range(1, plan.outer):
            self.first_copy(p, d).start()
        for e in range(1, plan.inner):
            self.second_copy(p, 0, e).start()

    def forward(self, p):
        plan = self.plan
        for d in range(1, plan.outer):
            self.first_copy(p, d).wait_recv()
            for e in range(1, plan.inner):
                self.second_copy(p, d, e).start()

    def arrive(self, p, d):
        plan = self.plan
        places = []
        for e in range(1, plan.inner):
            self.second_copy(p, d, e).wait_recv()
            places.append(plan.row(plan.o_at(plan.outer - d), plan.i_at(plan.inner - e)) * self.per + p)
        return places

    def finish(self):
        plan = self.plan
        for p in range(self.per):
            for d in range(1, plan.outer):
                self.first_copy(p, d).wait_send()
            for d in range(plan.outer):
                for e in range(1, plan.inner):
                    self.second_copy(p, d, e).wait_send()


def vmem():
    return pl.BlockSpec(memory_space=pltpu.VMEM)


def triangle():
    rows = lax.broadcasted_iota(jnp.int32, (TILE, TILE), 0)
    columns = lax.broadcasted_iota(jnp.int32, (TILE, TILE), 1)
    return rows, columns


def pairs(count):
    return [(i, j) for i in range(count) for j in range(i + 1, count)]


EXTRA = 16


def packed_rows(width):
    count = width // TILE
    return TILE * (len(pairs(count)) + count // 2) + EXTRA


def pack(tile):
    count = tile.count
    rows, columns = triangle()
    at = 0
    for i, j in pairs(count):
        yield at, tile(i, j).astype(BF16)
        at += TILE
    extra = lax.broadcasted_iota(jnp.int32, (EXTRA, TILE), 0)
    diagonals = jnp.zeros((EXTRA, TILE), F32)
    for k in range(0, count, 2):
        upper, lower = tile(k, k), tile(k + 1, k + 1)
        yield at, jnp.where(rows <= columns, upper, lower).astype(BF16)
        at += TILE
        diagonal = jnp.sum(jnp.where(rows == columns, lower, 0.0), axis=0, keepdims=True)
        diagonals = jnp.where(extra == k // 2, diagonal, diagonals)
    yield at, diagonals.astype(BF16)


class Tiles:
    def __init__(self, count, get):
        self.count, self.get = count, get

    def __call__(self, i, j):
        return self.get(i, j)


def unpack(packed, width, dtype):
    count = width // TILE
    rows, columns = triangle()
    tiles = {}
    at = 0
    for i, j in pairs(count):
        tile = packed[at : at + TILE].astype(dtype)
        tiles[i, j], tiles[j, i] = tile, tile.T
        at += TILE
    diagonals = packed[at + TILE * (count // 2) :].astype(F32)
    for k in range(0, count, 2):
        both = packed[at : at + TILE].astype(F32)
        other = both.T
        line = diagonals[k // 2 : k // 2 + 1]
        tiles[k, k] = jnp.where(rows <= columns, both, other).astype(dtype)
        lower = jnp.where(rows > columns, both, other)
        tiles[k + 1, k + 1] = jnp.where(rows == columns, line, lower).astype(dtype)
        at += TILE
    return jnp.concatenate(
        [jnp.concatenate([tiles[i, j] for j in range(count)], axis=1) for i in range(count)], axis=0
    )


def mm(a, b):
    return jnp.dot(a.astype(BF16), b.astype(BF16), preferred_element_type=F32)


def factors(gram):
    width = gram.shape[-1]
    rows = lax.broadcasted_iota(jnp.int32, (width, width), 0)
    columns = lax.broadcasted_iota(jnp.int32, (width, width), 1)
    diagonal = rows == columns
    first_eye = jnp.where(diagonal, coef_first, 0.0)
    squares = jnp.sum(jnp.where(diagonal, gram, 0.0), axis=0, keepdims=True)
    total = jnp.sum(squares, axis=1, keepdims=True)
    inverse = 1.0 / (jnp.sqrt(total) + epsilon)
    a = gram * inverse * inverse
    q = None
    for sweep in range(ITERS):
        poly = coef_second * a + coef_third * mm(a, a)
        q = first_eye + poly if q is None else coef_first * q + mm(q, poly)
        if sweep < ITERS - 1:
            half = coef_first * a + mm(a, poly)
            a = coef_first * half + mm(poly, half)
    return q * inverse


def store_gram(mom, s, x):
    fresh = mom[s]
    width = fresh.shape[1]
    lines = {}

    def tile(i, j):
        if i not in lines:
            lines[i] = lax.dot_general(
                fresh[:, i * TILE : (i + 1) * TILE],
                fresh[:, i * TILE :],
                (((0,), (0,)), ((), ())),
                preferred_element_type=F32,
            )
        return lines[i][:, (j - i) * TILE : (j - i + 1) * TILE]

    for at, piece in pack(Tiles(width // TILE, tile)):
        x[s, at : at + piece.shape[0]] = piece


def store_factors(value, width, s, out):
    q = factors(unpack(value, width, F32))

    def tile(i, j):
        return q[i * TILE : (i + 1) * TILE, j * TILE : (j + 1) * TILE]

    for at, piece in pack(Tiles(width // TILE, tile)):
        out[s, at : at + piece.shape[0]] = piece


def store_weights(mom, packed, s, out):
    scale_step = step_rate * 0.2 * math.sqrt(max(D, FF))
    full = unpack(packed[s], mom.shape[2], BF16)
    ortho = jnp.dot(mom[s], full, preferred_element_type=F32)
    kept = out[s].astype(F32) * (1.0 - step_rate * decay_rate)
    out[s] = (kept - scale_step * ortho).astype(BF16)


def store_projection(basis, grads, s, out):
    out[s] = jnp.dot(basis[s].astype(BF16), grads[s], preferred_element_type=F32).astype(BF16)


def store_momentum(flags, old, grads, basis, proj, s, mom):
    low = lax.dot_general(
        basis[s].astype(BF16), proj[s], (((0,), (0,)), ((), ())), preferred_element_type=F32
    )
    flag = residual_weight * flags[s].astype(F32)
    grad_full = grads[s].astype(F32)
    mom[s] = (momentum_decay * old[s].astype(F32) + low + flag * (grad_full - low)).astype(BF16)


def step_kernel(owners, per, flags, old, grads, basis, weights, mom, out, fetched, px, proj, x, packed, *scratch):
    width = mom.shape[2]
    fetch = pltpu.make_async_copy(weights, out, fetched)
    fetch.start()
    plan = Plan(owners)
    plan.barrier()
    proj_scatter = SumScatter(plan, per, px, *scratch[:2], scratch[2:6])
    proj_gather = Gather(plan, per, proj, scratch[6:10])
    scatter = SumScatter(plan, per, x, *scratch[10:12], scratch[12:16])
    gather = Gather(plan, per, packed, scratch[16:])
    outer, inner = plan.outer, plan.inner

    def project(p):
        @pl.loop(1, outer + 1)
        def _(later):
            d = lax.rem(later, outer)
            for e in range(1, inner):
                store_projection(basis, grads, plan.row(plan.o_at(d), plan.i_at(e)) * per + p, px)
                proj_scatter.first_copy(p, d, e).start()

    def project_own(p):
        @pl.loop(0, outer)
        def _(d):
            store_projection(basis, grads, plan.row(plan.o_at(d), plan.i) * per + p, px)

    def own_sum(p):
        proj[proj_gather.mine(p)] = proj_scatter.total(p).astype(BF16)
        proj_gather.start(p)

    def prepare(s):
        store_momentum(flags, old, grads, basis, proj, s, mom)
        store_gram(mom, s, x)

    def first(p):
        @pl.loop(1, outer + 1)
        def _(later):
            d = lax.rem(later, outer)
            for e in range(1, inner):
                prepare(plan.row(plan.o_at(d), plan.i_at(e)) * per + p)
                scatter.first_copy(p, d, e).start()

    def own(p):
        @pl.loop(0, outer)
        def _(d):
            prepare(plan.row(plan.o_at(d), plan.i) * per + p)

    def owner_work(p):
        store_factors(scatter.total(p), width, gather.mine(p), packed)
        gather.start(p)

    def last(p):
        for d in range(outer):
            store_weights(mom, packed, plan.row(plan.o_at(outer - d), plan.i) * per + p, out)
            for s in gather.arrive(p, d):
                store_weights(mom, packed, s, out)

    for p in range(per):
        project(p)
    for p in range(per):
        project_own(p)
    for p in range(per):
        proj_scatter.forward(p)
        if p:
            own_sum(p - 1)
    own_sum(per - 1)
    for p in range(per):
        proj_gather.forward(p)
    for p in range(per):
        for d in range(outer):
            proj_gather.arrive(p, d)
        first(p)
        if p == 0:
            own(0)
            scatter.forward_one(0, 1)
    for d in list(range(2, outer)) + [0]:
        scatter.forward_one(0, d)
    for p in range(1, per):
        own(p)
    for p in range(per):
        if p + 1 < per:
            scatter.forward_one(p + 1, 1)
        owner_work(p)
        if p + 1 < per:
            for d in list(range(2, outer)) + [0]:
                scatter.forward_one(p + 1, d)
            gather.forward(p)
    gather.forward(per - 1)
    fetch.wait()
    for p in range(per):
        last(p)
    proj_scatter.finish()
    proj_gather.finish()
    scatter.finish()
    gather.finish()


def step(refresh, old, grads, basis_t, weights, owners):
    count, rows, width = grads.shape
    per = count // owners
    tile = (packed_rows(width), TILE)
    line = (basis_t.shape[1], width)
    scratch = (
        [pltpu.SemaphoreType.DMA]
        + [pltpu.VMEM((count,) + line, BF16)] * 2
        + [pltpu.VMEM((count,) + tile, BF16)] * 2
        + SumScatter.scratch(owners, per, line)
        + Gather.scratch(owners, per)
        + SumScatter.scratch(owners, per, tile)
        + Gather.scratch(owners, per)
    )
    held = sum(2 * math.prod(one.shape) for one in scratch if one.dtype == BF16)
    return pl.pallas_call(
        functools.partial(step_kernel, owners, per),
        out_shape=(
            jax.ShapeDtypeStruct(weights.shape, BF16),
            jax.ShapeDtypeStruct(weights.shape, weights.dtype),
        ),
        in_specs=[pl.BlockSpec(memory_space=pltpu.SMEM)]
        + [vmem()] * 3
        + [pl.BlockSpec(memory_space=pltpu.HBM)],
        out_specs=(vmem(), vmem()),
        scratch_shapes=scratch,
        compiler_params=pltpu.CompilerParams(
            collective_id=0, has_side_effects=True, vmem_limit_bytes=held + SPARE
        ),
        name="step",
    )(refresh, old, grads, basis_t, weights)


def take_kernel(count, order, bank, new_bank, old, stage, came, went):
    total = bank.shape[0]

    def reading(j):
        target = old.at[j] if j < count else stage.at[j - count]
        return pltpu.make_async_copy(bank.at[order[j]], target, came.at[j])

    def writing(j):
        return pltpu.make_async_copy(stage.at[j - count], new_bank.at[order[j]], went.at[j - count])

    for j in list(range(count, total)) + list(range(count)):
        reading(j).start()
    for j in range(count, total):
        reading(j).wait()
        writing(j).start()
    for j in range(count):
        reading(j).wait()
    for j in range(count, total):
        writing(j).wait()


def take(order, bank, count):
    others = max(bank.shape[0] - count, 1)
    shape = bank.shape[1:]
    return pl.pallas_call(
        functools.partial(take_kernel, count),
        out_shape=(
            jax.ShapeDtypeStruct(bank.shape, bank.dtype),
            jax.ShapeDtypeStruct((count,) + shape, bank.dtype),
        ),
        in_specs=[pl.BlockSpec(memory_space=pltpu.SMEM), pl.BlockSpec(memory_space=pltpu.HBM)],
        out_specs=(pl.BlockSpec(memory_space=pltpu.HBM), vmem()),
        scratch_shapes=[
            pltpu.VMEM((others,) + shape, bank.dtype),
            pltpu.SemaphoreType.DMA((bank.shape[0],)),
            pltpu.SemaphoreType.DMA((others,)),
        ],
        compiler_params=pltpu.CompilerParams(vmem_limit_bytes=46 << 20),
        name="take",
    )(order, bank)


def put_kernel(order, kept, mom, new_bank, sems):
    def writing(j):
        return pltpu.make_async_copy(mom.at[j], new_bank.at[order[j]], sems.at[j])

    for j in range(mom.shape[0]):
        writing(j).start()
    for j in range(mom.shape[0]):
        writing(j).wait()


def put(order, kept, mom):
    return pl.pallas_call(
        put_kernel,
        out_shape=jax.ShapeDtypeStruct(kept.shape, kept.dtype),
        in_specs=[
            pl.BlockSpec(memory_space=pltpu.SMEM),
            pl.BlockSpec(memory_space=pltpu.HBM),
            vmem(),
        ],
        out_specs=pl.BlockSpec(memory_space=pltpu.HBM),
        scratch_shapes=[pltpu.SemaphoreType.DMA((mom.shape[0],))],
        input_output_aliases={1: 0},
        compiler_params=pltpu.CompilerParams(vmem_limit_bytes=1 << 20),
        name="put",
    )(order, kept, mom)


def shards(owners, sampled, refresh, momentum_bank, weights, grads, basis):
    order = sampled[0]
    kept, old = take(order, momentum_bank, weights.shape[0])
    mom, new_weights = step(refresh, old, grads, jnp.swapaxes(basis, 1, 2), weights, owners)
    return put(order, kept, mom), new_weights


def solution(mesh):
    in_specs = (
        P("expert", None),
        P("expert"),
        P("expert", "row", None),
        P("expert", "row", None),
        P("expert", "row", None),
        P("expert", "row", None),
    )
    out_specs = (P("expert", "row", None), P("expert", "row", None))
    return jax.shard_map(
        functools.partial(shards, mesh.shape["row"]),
        mesh=mesh,
        in_specs=in_specs,
        out_specs=out_specs,
        check_vma=False,
    )
```
